32 devices in a mesh: seq: 8 (over y, x, core), dp: 4 (over z).
Axes of the slice: x: 2, y: 2, z: 4, core: 2. Of those that a mesh axis runs over, the one named last changes fastest.
Arguments:
- queries: bfloat16 [4, 2048, 2048], P('dp', 'seq'), may hold values from -34 to 34
- key_heads: bfloat16 [4, 2048, 512], P('dp', 'seq'), may hold values from -7 to 7
- value_heads: bfloat16 [4, 2048, 512], P('dp', 'seq'), may hold values from -6 to 6
- doc_lengths: int32 [4, 16], P('dp'), may hold values from 1 to 256, 2048 in all within a row
- out_weight: bfloat16 [2048, 2048], P('dp'), may hold values from -0.125 to 0.125
- cotangent: bfloat16 [4, 2048, 2048], P('dp', 'seq'), may hold values from -6 to 6
Outputs:
- projected: bfloat16 [4, 2048, 2048], P('dp', 'seq')
- grad_queries: bfloat16 [4, 2048, 2048], P('dp', 'seq')
- grad_keys: bfloat16 [4, 2048, 512], P('dp', 'seq')
- grad_values: bfloat16 [4, 2048, 512], P('dp', 'seq')
- grad_weight: float32 [2048, 2048], P('dp')
The draws below stay inside these ranges and needn't reach their ends.
Inputs may be any that keep to these rules, and one draw needn't show every extreme that they name: `doc_lengths`: each pack's documents lie end to end in this order and fill its 2048 tokens; no document is longer than 256 tokens, and in every pack one document is exactly that long.
All inputs are finite; a program needn't handle non-finite values.
Results may differ from the reference program's by a relative error of at most 0.017.
Values may be sent and summed in bfloat16 or wider, within the bound.
No kernel may reach another device: no remote copies, remote signals or barrier semaphores. Data moves between devices by JAX's collectives and lax.ppermute only.
A program may use at most 128 MiB of HBM per device.

```python
import math
import jax
import jax.numpy as jnp
import numpy as np
from jax import lax

HQ = 16
HK = 4
DH = 128
DM = 2048
TOK_DEV = 256
QW = 2048
KW = 512
SEQ = 2048
PACKS = 4
DOCS = 16
N_SEQ = 8


def paired_draw(key):
    group = HQ // HK
    key_query = jax.random.fold_in(key, 101)
    key_key = jax.random.fold_in(key, 102)
    key_rows = jnp.clip(jax.random.normal(key_key, (PACKS, SEQ, HK, DH), jnp.float32), -6.0, 6.0)
    query_rows = jnp.clip(jax.random.normal(key_query, (PACKS, SEQ, HK, group, DH), jnp.float32), -6.0, 6.0)
    return (query_rows.reshape(PACKS, SEQ, HK * group * DH), key_rows.reshape(PACKS, SEQ, HK * DH))


def draw_queries(key, part):
    return paired_draw(key)[0].astype(jnp.bfloat16)


def draw_key_heads(key, part):
    return paired_draw(key)[1].astype(jnp.bfloat16)


def shard_levels(key, shape, pieces, smallest, largest):
    factor_of = 1.0
    for axis_at, blocks in pieces:
        steps = jax.random.uniform(jax.random.fold_in(jax.random.fold_in(key, 6), axis_at), (blocks,), jnp.float32, smallest / len(pieces), largest / len(pieces))
        factor_of = factor_of * jnp.repeat(jnp.exp(steps), shape[axis_at] // blocks).reshape((-1,) + (1,) * (len(shape) - 1 - axis_at))
    return factor_of


def split_up(number_of, total, bound, lean):
    weights = [(1 << 20) // math.isqrt(rank ** lean) + 1 for rank in range(2, number_of + 1)]
    spare, given = total - bound - (number_of - 1), [1] * (number_of - 1)
    while spare > 0:
        movable = [i for i in range(number_of - 1) if given[i] < bound]
        whole, budget = sum([weights[i] for i in movable]), spare
        for i in movable:
            more = min(bound - given[i], max(1, budget * weights[i] // whole), spare)
            given[i] = given[i] + more
            spare = spare - more
    return np.array([bound] + given)


def ragged(stream_key, count, total, bound, slope):
    if count == 2:
        one = jax.random.randint(stream_key, (), max(1, total - bound), min(bound, total - 1) + 1)
        return jnp.stack([one, total - one])
    tallies = jnp.asarray(split_up(count, total, bound, slope), jnp.int32)
    couples = (count - 1) // 2
    giver, taker = tallies[1:1 + 2 * couples:2], tallies[2:2 + 2 * couples:2]
    margin = jnp.minimum(giver - 1, bound - taker)
    moved = jax.random.randint(jax.random.fold_in(stream_key, 1), (couples,), 0, 1 << 20) % (margin + 1)
    tallies = tallies.at[1:1 + 2 * couples:2].set(giver - moved).at[2:2 + 2 * couples:2].set(taker + moved)
    return tallies[jax.random.permutation(jax.random.fold_in(stream_key, 2), count)]


def centred(own_key, shape, width, limit, pieces=(), kind=jnp.bfloat16):
    values = width * jax.random.normal(own_key, shape, jnp.float32)
    if pieces:
        values = values * shard_levels(own_key, shape, pieces, -0.22, 0.18)
    return jnp.clip(values, -limit, limit).astype(kind)


def setup_inputs(seed: int = 0) -> dict:
    streams_of = jax.random.split(jax.random.key(seed), 7)
    queries = draw_queries(jax.random.fold_in(streams_of[6], 71), 0)
    key_heads = draw_key_heads(jax.random.fold_in(streams_of[6], 71), 0)
    value_heads = centred(streams_of[2], (PACKS, SEQ, KW), 1.0, 6.0, ((0, 4), (1, 8)))
    doc_lengths = jax.vmap(lambda own: ragged(own, DOCS, SEQ, TOK_DEV, 1))(jax.random.split(streams_of[3], PACKS)).reshape((PACKS, DOCS)).astype(jnp.int32)
    out_weight = centred(streams_of[4], (QW, DM), QW ** -0.5, 0.125, ((0, 4),))
    cotangent = centred(streams_of[5], (PACKS, SEQ, DM), 1.0, 6.0, ((0, 4), (1, 8)))
    return {"queries": queries, "key_heads": key_heads, "value_heads": value_heads, "doc_lengths": doc_lengths, "out_weight": out_weight, "cotangent": cotangent}


def doc_begin(lengths, position):
    ending = jnp.cumsum(lengths).astype(jnp.int32)
    opening = (ending - lengths).astype(jnp.int32)
    covered = opening[None, :] <= position[:, None]
    return lax.optimization_barrier(jnp.max(jnp.where(covered, opening[None, :], 0), axis=-1)).astype(jnp.int32)

def attend_block(query, key_block, value_block, grad_att, q_begin, q_pos, k_pos):
    rows = query.shape[0]
    span = key_block.shape[0]
    group = HQ // HK
    scale = 1.0 / math.sqrt(DH)
    q_heads = query.reshape(rows, HK, group, DH).astype(jnp.float32)
    k_heads = key_block.reshape(span, HK, DH).astype(jnp.float32)
    v_heads = value_block.reshape(span, HK, DH).astype(jnp.float32)
    g_heads = grad_att.reshape(rows, HK, group, DH).astype(jnp.float32)
    scores = jnp.einsum('ikgd,jkd->kgij', q_heads, k_heads) * scale
    allowed = (k_pos[None, :] >= q_begin[:, None]) & (k_pos[None, :] <= q_pos[:, None])
    scores = jnp.where(allowed, scores, -jnp.inf)
    peak = lax.optimization_barrier(jnp.max(scores, axis=-1, keepdims=True))
    logsum = peak + jnp.log(lax.optimization_barrier(jnp.sum(jnp.exp(scores - peak), axis=-1, keepdims=True)))
    probs = jnp.exp(scores - logsum)
    probs_low = lax.optimization_barrier(probs.astype(jnp.bfloat16))
    attended = jnp.einsum('kgij,jkd->ikgd', probs_low.astype(jnp.float32), v_heads).astype(jnp.bfloat16)
    delta = jnp.einsum('ikgd,ikgd->kgi', g_heads, attended.astype(jnp.float32))
    grad_probs = jnp.einsum('ikgd,jkd->kgij', g_heads, v_heads)
    grad_low = lax.optimization_barrier((probs * (grad_probs - delta[..., None])).astype(jnp.bfloat16))
    grad_scores = grad_low.astype(jnp.float32)
    grad_query = (jnp.einsum('kgij,jkd->ikgd', grad_scores, k_heads) * scale).astype(jnp.bfloat16)
    grad_key = jnp.einsum('kgij,ikgd->jkd', grad_scores, q_heads) * scale
    grad_value = jnp.einsum('kgij,ikgd->jkd', probs_low.astype(jnp.float32), g_heads)
    return (attended.reshape(rows, HK * group * DH), grad_query.reshape(rows, HK * group * DH), grad_key.reshape(span, HK * DH), grad_value.reshape(span, HK * DH))

def reference(queries, key_heads, value_heads, doc_lengths, out_weight, cotangent):
    position = jnp.arange(SEQ, dtype=jnp.int32)

    def pack_begin(lengths):
        return doc_begin(lengths, position)
    begins = jax.vmap(pack_begin)(doc_lengths)
    flat_cot = cotangent.reshape(PACKS * SEQ, DM)
    grad_att = jnp.dot(flat_cot, out_weight.T, preferred_element_type=jnp.float32).astype(jnp.bfloat16)
    grad_att = grad_att.reshape(PACKS, SEQ, QW)
    padding = jnp.zeros((PACKS, TOK_DEV, KW), jnp.bfloat16)
    key_pad = jnp.concatenate([padding, key_heads], axis=1)
    value_pad = jnp.concatenate([padding, value_heads], axis=1)

    def one_block(index):
        pack = (index // N_SEQ).astype(jnp.int32)
        block = (index % N_SEQ).astype(jnp.int32)
        offset = (block * TOK_DEV).astype(jnp.int32)

        def select(array):
            return lax.dynamic_index_in_dim(array, pack, 0, keepdims=False)
        query = lax.dynamic_slice_in_dim(select(queries), offset, TOK_DEV, 0)
        key_block = lax.dynamic_slice_in_dim(select(key_pad), offset, 2 * TOK_DEV, 0)
        value_block = lax.dynamic_slice_in_dim(select(value_pad), offset, 2 * TOK_DEV, 0)
        grad_block = lax.dynamic_slice_in_dim(select(grad_att), offset, TOK_DEV, 0)
        q_begin = lax.dynamic_slice_in_dim(select(begins), offset, TOK_DEV, 0)
        q_pos = (offset + jnp.arange(TOK_DEV, dtype=jnp.int32)).astype(jnp.int32)
        k_pos = (offset - TOK_DEV + jnp.arange(2 * TOK_DEV, dtype=jnp.int32)).astype(jnp.int32)
        return attend_block(query, key_block, value_block, grad_block, q_begin, q_pos, k_pos)
    attended, grad_q, grad_k, grad_v = lax.map(one_block, jnp.arange(PACKS * N_SEQ, dtype=jnp.int32))

    def settle(part):
        part = part.reshape(PACKS, N_SEQ, 2 * TOK_DEV, KW)
        earlier = part[:, :, :TOK_DEV]
        own_part = part[:, :, TOK_DEV:]
        carried = jnp.concatenate([earlier[:, 1:], jnp.zeros_like(earlier[:, :1])], axis=1)
        return (own_part + carried).astype(jnp.bfloat16).reshape(PACKS, SEQ, KW)
    attended = attended.reshape(PACKS * SEQ, QW)
    projected = jnp.dot(attended, out_weight, preferred_element_type=jnp.float32).astype(jnp.bfloat16)
    grad_weight = jnp.dot(attended.T, flat_cot, preferred_element_type=jnp.float32) * (1.0 / math.sqrt(PACKS * SEQ))
    return (projected.reshape(PACKS, SEQ, DM), grad_q.reshape(PACKS, SEQ, QW), settle(grad_k), settle(grad_v), grad_weight)
```

```python
import functools
import math

import jax
import jax.numpy as jnp
from jax import lax
from jax.experimental import pallas as pl
from jax.experimental.pallas import tpu as pltpu
from jax.sharding import PartitionSpec as P

HQ = 16
HK = 4
DH = 128
GROUP = HQ // HK
GW = GROUP * DH


BF = jnp.bfloat16
F32 = jnp.float32
ANY = pl.BlockSpec(memory_space=pl.ANY)
VM = pl.BlockSpec(memory_space=pltpu.VMEM)
SM = pl.BlockSpec(memory_space=pltpu.SMEM)


def mm(a, b):
    return jnp.dot(a, b, preferred_element_type=F32)


def mm_nt(a, b):
    return lax.dot_general(a, b, (((1,), (1,)), ((), ())), preferred_element_type=F32)


def mm_tn(a, b):
    return lax.dot_general(a, b, (((0,), (0,)), ((), ())), preferred_element_type=F32)


def cost(flops, nbytes, trans=0):
    return pl.CostEstimate(flops=int(flops), bytes_accessed=int(nbytes), transcendentals=int(trans))


def stacked(block, low, size):
    return jnp.concatenate(
        [block[low : low + size, h * DH : (h + 1) * DH] for h in range(GROUP)], axis=0
    )


def forward_kernel(lens, first, q_ref, halo_ref, k_ref, v_ref, att_ref, att_t_ref, p_ref, bias):
    rows = q_ref.shape[0]
    half = rows // 2
    span = rows + half

    @pl.when(pl.program_id(0) == 0)
    def _():
        for a in range(2):
            base = first[0] + a * half
            q_pos = base + lax.broadcasted_iota(jnp.int32, (span, half), 1)
            k_pos = base - rows + lax.broadcasted_iota(jnp.int32, (span, half), 0)
            begin = jnp.zeros((span, half), jnp.int32)
            opening = jnp.int32(0)
            for i in range(lens.shape[1]):
                begin = jnp.where(opening <= q_pos, opening, begin)
                opening = opening + lens[0, i]
            allowed = (k_pos >= begin) & (k_pos <= q_pos)
            bias[a] = jnp.where(allowed, 0.0, -jnp.inf).astype(F32)

    keys = jnp.concatenate([halo_ref[0], k_ref[...]], axis=0)
    values = jnp.concatenate([halo_ref[1], v_ref[...]], axis=0)
    block = q_ref[...]
    factor = math.log2(math.e) / math.sqrt(DH)
    for a in range(2):
        part = slice(a * half, a * half + span)
        s = mm_nt(keys[part], stacked(block, a * half, half))
        s = s + jnp.concatenate([bias[a]] * GROUP, axis=1)
        e = jnp.exp2((s - jnp.max(s, axis=0, keepdims=True)) * factor)
        p = (e * (1.0 / jnp.sum(e, axis=0, keepdims=True))).astype(BF)
        p_ref[0, a] = p
        out_t = mm_tn(values[part], p)
        for h in range(GROUP):
            piece = out_t[:, h * half : (h + 1) * half]
            att_t_ref[h * DH : (h + 1) * DH, a * half : (a + 1) * half] = piece.astype(BF)
            att_ref[a * half : (a + 1) * half, h * DH : (h + 1) * DH] = piece.T.astype(BF)


def forward(lens, first, query, halo, keys, values):
    rows = query.shape[0]
    span = rows + rows // 2
    head = lambda g: (0, g)
    return pl.pallas_call(
        forward_kernel,
        grid=(HK,),
        in_specs=[
            SM,
            SM,
            pl.BlockSpec((rows, GW), head),
            pl.BlockSpec((2, rows, DH), lambda g: (0, 0, g)),
            pl.BlockSpec((rows, DH), head),
            pl.BlockSpec((rows, DH), head),
        ],
        out_specs=[
            pl.BlockSpec((rows, GW), head),
            pl.BlockSpec((GW, rows), lambda g: (g, 0)),
            pl.BlockSpec((1, 2, span, GW), lambda g: (g, 0, 0, 0)),
        ],
        out_shape=[
            jax.ShapeDtypeStruct(query.shape, BF),
            jax.ShapeDtypeStruct(query.shape[::-1], BF),
            jax.ShapeDtypeStruct((HK, 2, span, GW), BF),
        ],
        scratch_shapes=[pltpu.VMEM((2, span, rows // 2), F32)],
        cost_estimate=cost(4 * HK * 2 * span * GW * DH, 8 << 20, HK * 2 * span * GW),
        name="attend_forward",
    )(lens, first, query, halo, keys, values)


def backward_kernel(q_ref, g_ref, halo_ref, k_ref, v_ref, p_ref, dq_ref, back_ref, dk_ref, dv_ref):
    rows = q_ref.shape[0]
    half = rows // 2
    span = rows + half
    scale = 1.0 / math.sqrt(DH)
    keys = jnp.concatenate([halo_ref[0], k_ref[...]], axis=0)
    values = jnp.concatenate([halo_ref[1], v_ref[...]], axis=0)
    block, grads = q_ref[...], g_ref[...]
    key_parts, value_parts = [], []
    for a in range(2):
        part = slice(a * half, a * half + span)
        qs, gs = stacked(block, a * half, half), stacked(grads, a * half, half)
        low = p_ref[0, a]
        p = low.astype(F32)
        dp = mm_nt(values[part], gs)
        delta = jnp.sum(p * dp, axis=0, keepdims=True)
        ds = (p * (dp - delta)).astype(BF)
        key_parts.append(mm(ds, qs) * scale)
        value_parts.append(mm(low, gs))
        out_t = mm_tn(keys[part], ds) * scale
        for h in range(GROUP):
            piece = out_t[:, h * half : (h + 1) * half]
            dq_ref[a * half : (a + 1) * half, h * DH : (h + 1) * DH] = piece.T.astype(BF)
    for which, (parts, own) in enumerate(((key_parts, dk_ref), (value_parts, dv_ref))):
        early, late = parts
        back_ref[which, :half] = early[:half].astype(BF)
        back_ref[which, half:] = (early[half:rows] + late[:half]).astype(BF)
        own[:half] = early[rows:] + late[half:rows]
        own[half:] = late[rows:]


def backward(query, grads, halo, keys, values, probs):
    rows = query.shape[0]
    span = rows + rows // 2
    head = lambda g: (0, g)
    pair = pl.BlockSpec((2, rows, DH), lambda g: (0, 0, g))
    thin = pl.BlockSpec((rows, DH), head)
    wide = pl.BlockSpec((rows, GW), head)
    return pl.pallas_call(
        backward_kernel,
        grid=(HK,),
        in_specs=[
            wide,
            wide,
            pair,
            thin,
            thin,
            pl.BlockSpec((1, 2, span, GW), lambda g: (g, 0, 0, 0)),
        ],
        out_specs=[wide, pair, thin, thin],
        out_shape=[
            jax.ShapeDtypeStruct(query.shape, BF),
            jax.ShapeDtypeStruct(halo.shape, BF),
            jax.ShapeDtypeStruct(keys.shape, F32),
            jax.ShapeDtypeStruct(keys.shape, F32),
        ],
        cost_estimate=cost(8 * HK * 2 * span * GW * DH, 8 << 20),
        name="attend_backward",
    )(query, grads, halo, keys, values, probs)


def block_grad_kernel(where, cot_ref, *rest):
    pieces = len(rest) - 4
    sources, (_, out_ref, block, sems) = rest[:pieces], rest[pieces:]
    depth = block.shape[0] // pieces
    copies = [
        pltpu.make_async_copy(
            sources[i],
            block.at[pl.ds(pl.multiple_of(where[1 + i] * depth, depth), depth)],
            sems.at[i],
        )
        for i in range(pieces)
    ]
    for copy in copies:
        copy.start()
    for copy in copies:
        copy.wait()
    out_ref[...] = mm_nt(cot_ref[...], block[...]).astype(BF)


def block_grad(where, cot, pieces, total):
    rows, width = cot.shape
    height = sum(piece.shape[0] for piece in pieces)
    return pl.pallas_call(
        block_grad_kernel,
        grid_spec=pltpu.PrefetchScalarGridSpec(
            num_scalar_prefetch=1,
            grid=(1,),
            in_specs=[pl.BlockSpec((rows, width), lambda i, w: (0, 0))]
            + [ANY] * (len(pieces) + 1),
            out_specs=pl.BlockSpec((rows, height), lambda i, w: (0, w[0])),
            scratch_shapes=[
                pltpu.VMEM((height, width), BF),
                pltpu.SemaphoreType.DMA((len(pieces),)),
            ],
        ),
        out_shape=jax.ShapeDtypeStruct(total.shape, BF),
        input_output_aliases={len(pieces) + 2: 0},
        cost_estimate=cost(2 * rows * width * height, 2 * width * (height + rows)),
        name="block_grad",
    )(where, cot, *pieces, total)


def project_kernel(counts, where, att_ref, *rest):
    sources, (out_ref, weight, total, sems) = rest[:-4], rest[-4:]
    height = weight.shape[1]
    copies, at = [], 0
    for block, count in enumerate(counts):
        depth = height // count
        group = []
        for i in range(count):
            spot = pl.multiple_of(where[block, 1 + i] * depth, depth)
            group.append(
                pltpu.make_async_copy(
                    sources[at], weight.at[block, pl.ds(spot, depth)], sems.at[at]
                )
            )
            at += 1
        copies.append(group)
    for group in copies:
        for copy in group:
            copy.start()
    tile = 512
    for block, group in enumerate(copies):
        for copy in group:
            copy.wait()
        spot = pl.multiple_of(where[block, 0] * height, 128)
        left = att_ref[:, pl.ds(spot, height)]
        last = block == len(copies) - 1
        for t in range(0, out_ref.shape[1], tile):
            cols = slice(t, t + tile)
            more = mm(left, weight[block, :, cols])
            if block:
                more = total[:, cols] + more
            if last:
                out_ref[:, cols] = more.astype(BF)
            else:
                total[:, cols] = more


def project(where, att, blocks):
    rows = att.shape[0]
    width = blocks[0][0].shape[1]
    height = sum(piece.shape[0] for piece in blocks[0])
    pieces = [piece for block in blocks for piece in block]
    return pl.pallas_call(
        functools.partial(project_kernel, tuple(len(block) for block in blocks)),
        in_specs=[SM, VM] + [ANY] * len(pieces),
        out_specs=VM,
        scratch_shapes=[
            pltpu.VMEM((len(blocks), height, width), BF),
            pltpu.VMEM((rows, width), F32),
            pltpu.SemaphoreType.DMA((len(pieces),)),
        ],
        out_shape=jax.ShapeDtypeStruct((rows, width), BF),
        cost_estimate=cost(2 * rows * width * att.shape[1], 2 * width * (att.shape[1] + rows)),
        name="project",
    )(where, att, *pieces)


def weight_grad_kernel(sources, added, where, *refs):
    lefts, rights = refs[:sources], refs[sources : 2 * sources]
    outs = refs[2 * sources + added :]
    depth = lefts[0].shape[0] // len(outs)
    for r, out in enumerate(outs):
        spot = where[1 + r] * depth if len(outs) > 1 else 0
        rows = pl.ds(pl.multiple_of(spot, depth), depth)
        total = mm(lefts[0][rows], rights[0][...])
        for left, right in zip(lefts[1:], rights[1:]):
            total += mm(left[rows], right[...])
        for extra in refs[2 * sources : 2 * sources + added]:
            total += extra[rows].astype(F32)
        out[...] = total.astype(BF)


def weight_grad(where, lefts, rights, extras, cols, pieces):
    height, tokens = lefts[0].shape
    full = lambda shape: pl.BlockSpec(shape, lambda i, w: (0, 0))
    return pl.pallas_call(
        functools.partial(weight_grad_kernel, len(lefts), len(extras)),
        grid_spec=pltpu.PrefetchScalarGridSpec(
            num_scalar_prefetch=1,
            grid=(1,),
            in_specs=[full((height, tokens))] * len(lefts)
            + [pl.BlockSpec((tokens, cols), lambda i, w: (0, w[0]))] * len(rights)
            + [full((height, cols))] * len(extras),
            out_specs=[full((height // pieces, cols))] * pieces,
        ),
        out_shape=[jax.ShapeDtypeStruct((height // pieces, cols), BF)] * pieces,
        cost_estimate=cost(
            2 * height * cols * tokens * len(lefts), 2 * len(lefts) * tokens * (height + cols)
        ),
        name="weight_grad",
    )(where, *lefts, *rights, *extras)


def spread_kernel(factor, where, *refs):
    pieces, out_ref = refs[:-1], refs[-1]
    depth, cols = pieces[0].shape
    for i, piece in enumerate(pieces):
        row = pl.multiple_of(where[i, 0] * depth, depth)
        col = pl.multiple_of(where[i, 1] * cols, cols)
        out_ref[pl.ds(row, depth), pl.ds(col, cols)] = piece[...].astype(F32) * factor


def spread(factor, where, pieces, shape):
    return pl.pallas_call(
        functools.partial(spread_kernel, factor),
        in_specs=[SM] + [VM] * len(pieces),
        out_specs=VM,
        out_shape=jax.ShapeDtypeStruct(shape, F32),
        cost_estimate=cost(shape[0] * shape[1], 6 * shape[0] * shape[1]),
        name="spread",
    )(where, *pieces)


def body(queries, key_heads, value_heads, doc_lengths, out_weight, cotangent):
    packs_here, rows, width = queries.shape
    assert packs_here == 1
    query, keys, values, cot = queries[0], key_heads[0], value_heads[0], cotangent[0]
    n = lax.axis_size("dp")
    m = lax.axis_size("seq")
    ny = m // 4
    assert m % 8 == 0
    d = lax.axis_index("dp")
    s = lax.axis_index("seq")
    core, x, y = s & 1, (s >> 1) & 1, s >> 2
    top = (s >= m // 2).astype(jnp.int32)

    def along(value, to):
        return lax.ppermute(value, "seq", [(i, to(i)) for i in range(m)])

    def behind(value, k):
        return lax.ppermute(value, "dp", [(i, (i - k) % n) for i in range(n)])

    def swap(value):
        return along(value, lambda i: i ^ 1)

    halo = lax.ppermute(
        jnp.stack([keys, values]), "seq", [(i, i + 1) for i in range(m - 1)]
    )

    height, dm = out_weight.shape
    quarter = height // 4
    first_bit = jnp.where(core == 0, top, x)
    other_bit = jnp.where(core == 0, x, top)
    mine = 2 * core + first_bit
    passed = 2 * core + 1 - first_bit
    theirs = 2 * (1 - core) + other_bit
    theirs_passed = 2 * (1 - core) + 1 - other_bit
    piece = lax.dynamic_slice(out_weight, (mine * quarter, 0), (quarter, dm))
    order = sorted(range(1, n), key=lambda k: min(k, n - k))
    taken = {k: behind(piece, k) for k in order}
    share = lambda i: i ^ (m // 2) if i % 2 == 0 else i ^ 2
    blocks, where = [[out_weight]], [[d, 0, 0, 0, 0]]
    for k in order:
        got = taken[k]
        more = along(got, share)
        blocks.append([got, more, swap(got), swap(more)])
        where.append([(d + k) % n, mine, passed, theirs, theirs_passed])
    where = [jnp.stack([jnp.asarray(v, jnp.int32) for v in row]) for row in where]

    first = (s * rows).astype(jnp.int32).reshape(1)
    att, att_t, probs = forward(doc_lengths, first, query, halo, keys, values)

    late_cot = cot
    cots = [cot, swap(late_cot), along(late_cot, lambda i: i ^ 2)]
    cots.append(swap(cots[2]))
    split = att_t.reshape(n, 4, quarter, rows)
    lane = 2 * x + core

    def rows_of(which):
        return lax.dynamic_index_in_dim(split, which, 1, keepdims=False).reshape(
            n * quarter, rows
        )

    lefts = [rows_of(lane)]
    for mask in (1, 2, 3):
        lefts.append(along(rows_of(lane ^ mask), lambda i, mask=mask: i ^ mask))
    cols = dm // ny
    shift = jnp.arange(n, dtype=jnp.int32)
    order_in = jnp.concatenate([jnp.zeros((1,), jnp.int32), (d + shift) % n]).astype(jnp.int32)
    arrived = []
    for j in range(1, ny):
        far = ((y + j) % ny).astype(jnp.int32)
        (part,) = weight_grad(order_in.at[0].set(far), lefts, cots, [], cols, 1)
        arrived.append(along(part, lambda i, j=j: (i + 4 * j) % m))
    sums = weight_grad(order_in.at[0].set(y.astype(jnp.int32)), lefts, cots, arrived, cols, n)
    total = sums[0].astype(F32)
    for k in range(1, n):
        total = total + lax.ppermute(
            sums[k], "dp", [(i, (i + k) % n) for i in range(n)]
        ).astype(F32)
    final = total.astype(BF)
    finals, places = [], []
    for dy in range(ny):
        for dx in range(2):
            to = lambda i, dx=dx, dy=dy: ((i ^ (2 * dx)) - 4 * dy) % m
            here = final if dx == 0 and dy == 0 else along(final, to)
            spot_y, spot_x = (y + dy) % ny, x ^ dx
            finals += [here, swap(here)]
            places += [(2 * spot_x + core, spot_y), (2 * spot_x + 1 - core, spot_y)]
    places = jnp.stack(
        [jnp.stack([jnp.asarray(v, jnp.int32) for v in place]) for place in places]
    )
    factor = 1.0 / math.sqrt(n * rows * m)
    grad_weight = spread(factor, places, finals, out_weight.shape)

    grad_att = jnp.zeros((rows, width), BF)
    for at, block in zip(where, blocks):
        grad_att = block_grad(at, cot, block, grad_att)
    grad_query, back, own_keys, own_values = backward(
        query, grad_att, halo, keys, values, probs
    )
    returned = lax.ppermute(back, "seq", [(i, i - 1) for i in range(1, m)])
    grad_keys = (own_keys + returned[0]).astype(BF)
    grad_values = (own_values + returned[1]).astype(BF)
    projected = project(jnp.stack(where), att, blocks)
    return tuple(
        a[None] for a in (projected, grad_query, grad_keys, grad_values)
    ) + (grad_weight,)


def solution(mesh):
    token = P("dp", "seq", None)
    return jax.shard_map(
        body,
        mesh=mesh,
        in_specs=(token, token, token, P("dp", None), P("dp", None), token),
        out_specs=(token, token, token, token, P("dp", None)),
        check_vma=False,
    )
```

```python
import functools
import math

import jax
import jax.numpy as jnp
from jax import lax
from jax.experimental import pallas as pl
from jax.experimental.pallas import tpu as pltpu
from jax.sharding import PartitionSpec as P


HQ = 16
HK = 4
DH = 128
GROUP = HQ // HK
GW = GROUP * DH


BF = jnp.bfloat16
ROOM = 24 << 20
F32 = jnp.float32
ANY = pl.BlockSpec(memory_space=pl.ANY)
VM = pl.BlockSpec(memory_space=pltpu.VMEM)
SM = pl.BlockSpec(memory_space=pltpu.SMEM)


def mm(a, b):
    return jnp.dot(a, b, preferred_element_type=F32)


def mm_nt(a, b):
    return lax.dot_general(a, b, (((1,), (1,)), ((), ())), preferred_element_type=F32)


def mm_tn(a, b):
    return lax.dot_general(a, b, (((0,), (0,)), ((), ())), preferred_element_type=F32)


def cost(flops, nbytes, trans=0):
    return pl.CostEstimate(flops=int(flops), bytes_accessed=int(nbytes), transcendentals=int(trans))


def stacked(block, low, size):
    return jnp.concatenate(
        [block[low : low + size, h * DH : (h + 1) * DH] for h in range(GROUP)], axis=0
    )


def forward_kernel(split, lens, place, q_ref, early_ref, k_ref, v_ref, *refs):
    att_ref, p_ref, sets, (bias, whole) = refs[0], refs[1], refs[2:4], refs[4:]
    rows = q_ref.shape[0]
    half = rows // 2
    span = rows + half

    @pl.when(pl.program_id(0) == 0)
    def _():
        for a in range(2):
            base = place[0] + a * half
            q_pos = base + lax.broadcasted_iota(jnp.int32, (span, half), 1)
            k_pos = base - rows + lax.broadcasted_iota(jnp.int32, (span, half), 0)
            begin = jnp.zeros((span, half), jnp.int32)
            opening = jnp.int32(0)
            for i in range(lens.shape[1]):
                begin = jnp.where(opening <= q_pos, opening, begin)
                opening = opening + lens[0, i]
            allowed = (k_pos >= begin) & (k_pos <= q_pos)
            bias[a] = jnp.where(allowed, 0.0, -jnp.inf).astype(F32)

    keys = jnp.concatenate([early_ref[0], k_ref[...]], axis=0)
    values = jnp.concatenate([early_ref[1], v_ref[...]], axis=0)
    block = q_ref[...]
    factor = math.log2(math.e) / math.sqrt(DH)
    for a in range(2):
        part = slice(a * half, a * half + span)
        s = mm_nt(keys[part], stacked(block, a * half, half))
        s = s + jnp.concatenate([bias[a]] * GROUP, axis=1)
        e = jnp.exp2((s - jnp.max(s, axis=0, keepdims=True)) * factor)
        p = (e * (1.0 / jnp.sum(e, axis=0, keepdims=True))).astype(BF)
        p_ref[0, a] = p
        out_t = mm_tn(values[part], p)
        for h in range(GROUP):
            piece = out_t[:, h * half : (h + 1) * half]
            whole[h * DH : (h + 1) * DH, a * half : (a + 1) * half] = piece.astype(BF)
            att_ref[a * half : (a + 1) * half, h * DH : (h + 1) * DH] = piece.T.astype(BF)
    height = GW // split
    quarter = height // 4
    for far_x, out in enumerate(sets):
        for c in range(2):
            for t in range(split):
                at = t * height + (2 * (place[1] ^ far_x) + c) * quarter
                out[c, t * quarter : (t + 1) * quarter] = whole[
                    pl.ds(pl.multiple_of(at, quarter), quarter)
                ]


def forward(split, lens, place, query, early, keys, values):
    rows, width = query.shape
    span = rows + rows // 2
    head = lambda g: (0, g)
    thin = pl.BlockSpec((rows, DH), head)
    return pl.pallas_call(
        functools.partial(forward_kernel, split),
        grid=(HK,),
        in_specs=[
            SM,
            SM,
            pl.BlockSpec((rows, GW), head),
            pl.BlockSpec((2, rows, DH), lambda g: (0, 0, g)),
            thin,
            thin,
        ],
        out_specs=[
            pl.BlockSpec((rows, GW), head),
            pl.BlockSpec((1, 2, span, GW), lambda g: (g, 0, 0, 0)),
        ]
        + [pl.BlockSpec((2, GW // 4, rows), lambda g: (0, g, 0))] * 2,
        out_shape=[
            jax.ShapeDtypeStruct(query.shape, BF),
            jax.ShapeDtypeStruct((HK, 2, span, GW), BF),
        ]
        + [jax.ShapeDtypeStruct((2, width // 4, rows), BF)] * 2,
        scratch_shapes=[pltpu.VMEM((2, span, rows // 2), F32), pltpu.VMEM((GW, rows), BF)],
        cost_estimate=cost(4 * HK * 2 * span * GW * DH, 8 << 20, HK * 2 * span * GW),
        compiler_params=pltpu.CompilerParams(vmem_limit_bytes=ROOM),
        name="attend_forward",
    )(lens, place, far(query), early, far(keys), far(values))


def units_kernel(sizes, spots, info, cot_ref, q_ref, early_ref, k_ref, v_ref, p_ref, *refs):
    pieces = refs[: len(sizes)]
    dq_ref, back_ref, own_ref, weights, sems = refs[-5:]
    step = pl.program_id(0)

    @pl.when(step == 0)
    def _():
        copies = []
        for i, size in enumerate(sizes):
            spot = pl.multiple_of(info[spots + i] * size, size)
            copies.append(
                pltpu.make_async_copy(pieces[i], weights.at[pl.ds(spot, size)], sems.at[i])
            )
        for copy in copies:
            copy.start()
        for copy in copies:
            copy.wait()

    weight = weights.at[pl.ds(pl.multiple_of(step * GW, GW), GW)]
    rows = q_ref.shape[0]
    half = rows // 2
    span = rows + half
    scale = 1.0 / math.sqrt(DH)
    grads = mm_nt(cot_ref[...], weight[...]).astype(BF)
    keys = jnp.concatenate([early_ref[0], k_ref[...]], axis=0)
    values = jnp.concatenate([early_ref[1], v_ref[...]], axis=0)
    block = q_ref[...]
    key_parts, value_parts = [], []
    for a in range(2):
        part = slice(a * half, a * half + span)
        qs, gs = stacked(block, a * half, half), stacked(grads, a * half, half)
        low = p_ref[0, a]
        p = low.astype(F32)
        dp = mm_nt(values[part], gs)
        delta = jnp.sum(p * dp, axis=0, keepdims=True)
        ds = (p * (dp - delta)).astype(BF)
        key_parts.append(mm(ds, qs) * scale)
        value_parts.append(mm(low, gs))
        out_t = mm_tn(keys[part], ds) * scale
        for h in range(GROUP):
            piece = out_t[:, h * half : (h + 1) * half]
            dq_ref[a * half : (a + 1) * half, h * DH : (h + 1) * DH] = piece.T.astype(BF)
    for which, (early, late) in enumerate((key_parts, value_parts)):
        back_ref[0, which, :half] = early[:half].astype(BF)
        back_ref[0, which, half:] = (early[half:rows] + late[:half]).astype(BF)
        own_ref[0, which, :half] = early[rows:] + late[half:rows]
        own_ref[0, which, half:] = late[rows:]


def units(
    info, heads, spots, low, high, skip, count, cot, query, early, keys, values, probs, pieces,
    links
):
    rows, width = cot.shape
    span = rows + rows // 2
    steps = high - low
    head = lambda i, w: w[heads + low + i]
    full = pl.BlockSpec((rows, width), lambda i, w: (0, 0))
    wide = pl.BlockSpec((rows, GW), lambda i, w: (0, head(i, w)))
    thin = pl.BlockSpec((rows, DH), lambda i, w: (0, head(i, w)))
    pair = pl.BlockSpec((1, 2, rows, DH), lambda i, w: (i, 0, 0, 0))
    later = pl.BlockSpec((1, 2, rows, DH), lambda i, w: (i + low - skip, 0, 0, 0))
    both = pl.BlockSpec((2, rows, DH), lambda i, w: (0, 0, head(i, w)))
    sizes = tuple(piece.shape[0] for piece in pieces)
    return pl.pallas_call(
        functools.partial(units_kernel, sizes, spots),
        grid_spec=pltpu.PrefetchScalarGridSpec(
            num_scalar_prefetch=1,
            grid=(steps,),
            in_specs=[full, wide, both, thin, thin]
            + [pl.BlockSpec((1, 2, span, GW), lambda i, w: (head(i, w), 0, 0, 0))]
            + [ANY] * (len(pieces) + len(links)),
            out_specs=[wide, later, pair],
            scratch_shapes=[
                pltpu.VMEM((steps * GW, width), BF),
                pltpu.SemaphoreType.DMA((len(pieces),)),
            ],
        ),
        out_shape=[
            jax.ShapeDtypeStruct(query.shape, BF),
            jax.ShapeDtypeStruct((count, 2, rows, DH), BF),
            jax.ShapeDtypeStruct((steps, 2, rows, DH), F32),
        ],
        input_output_aliases={7 + len(pieces) + i: i for i in range(len(links))},
        cost_estimate=cost(
            steps * (2 * rows * GW * width + 8 * 2 * span * GW * DH), steps * (5 << 20)
        ),
        compiler_params=pltpu.CompilerParams(vmem_limit_bytes=ROOM),
        name="units",
    )(info, far(cot), far(query), early, far(keys), far(values), probs, *pieces, *links)


def project_kernel(sizes, heads, spots, info, att_ref, *refs):
    pieces, (out_ref, weights, sems) = refs[: len(sizes)], refs[len(sizes) :]
    copies = []
    for i, size in enumerate(sizes):
        spot = pl.multiple_of(info[spots + i] * size, size)
        copies.append(
            pltpu.make_async_copy(pieces[i], weights.at[pl.ds(spot, size)], sems.at[i])
        )
    for copy in copies:
        copy.start()
    for copy in copies:
        copy.wait()
    lefts = [
        att_ref[:, pl.ds(pl.multiple_of(info[heads + u] * GW, GW), GW)] for u in range(HK)
    ]
    tile = 512
    for t in range(0, out_ref.shape[1], tile):
        value = mm(lefts[0], weights[:GW, t : t + tile])
        for u in range(1, HK):
            value += mm(lefts[u], weights[u * GW : (u + 1) * GW, t : t + tile])
        out_ref[:, t : t + tile] = value.astype(BF)


def project(info, heads, spots, att, pieces):
    rows, depth = att.shape
    width = pieces[0].shape[1]
    sizes = tuple(piece.shape[0] for piece in pieces)
    return pl.pallas_call(
        functools.partial(project_kernel, sizes, heads, spots),
        in_specs=[SM, VM] + [ANY] * len(pieces),
        out_specs=VM,
        out_shape=jax.ShapeDtypeStruct((rows, width), BF),
        scratch_shapes=[
            pltpu.VMEM((depth, width), BF),
            pltpu.SemaphoreType.DMA((len(pieces),)),
        ],
        cost_estimate=cost(2 * rows * depth * width, 2 * width * (depth + rows)),
        compiler_params=pltpu.CompilerParams(vmem_limit_bytes=ROOM),
        name="project",
    )(info, att, *pieces)


def both_kernel(k_ref, v_ref, out_ref):
    out_ref[0] = k_ref[...]
    out_ref[1] = v_ref[...]


def both(keys, values):
    return pl.pallas_call(
        both_kernel,
        in_specs=[VM, VM],
        out_specs=VM,
        out_shape=jax.ShapeDtypeStruct((2,) + keys.shape, BF),
        cost_estimate=cost(0, 8 * keys.size),
        compiler_params=pltpu.CompilerParams(vmem_limit_bytes=ROOM),
        name="both",
    )(far(keys), far(values))


def prepare_kernel(info, cot_ref, half_ref, quarter_ref, *outs):
    outs[0][...] = half_ref[...]
    outs[1][...] = quarter_ref[...]
    cols = outs[2].shape[1]
    count = len(outs) - 2
    for dy, out in enumerate(outs[2:]):
        which = lax.rem(info[3] + count - dy, count)
        out[...] = cot_ref[:, pl.ds(pl.multiple_of(which * cols, cols), cols)]


def prepare(info, cot, weight, ny):
    rows, width = cot.shape
    half, quarter = weight.shape[0] // 2, weight.shape[0] // 4
    still = lambda i, w: (0, 0)
    return pl.pallas_call(
        prepare_kernel,
        grid_spec=pltpu.PrefetchScalarGridSpec(
            num_scalar_prefetch=1,
            grid=(1,),
            in_specs=[
                pl.BlockSpec((rows, width), still),
                pl.BlockSpec((half, width), lambda i, w: (w[4], 0)),
                pl.BlockSpec((quarter, width), lambda i, w: (w[5], 0)),
            ],
            out_specs=[
                pl.BlockSpec((half, width), still),
                pl.BlockSpec((quarter, width), still),
            ]
            + [pl.BlockSpec((rows, width // ny), still)] * ny,
        ),
        out_shape=[
            jax.ShapeDtypeStruct((half, width), BF),
            jax.ShapeDtypeStruct((quarter, width), BF),
        ]
        + [jax.ShapeDtypeStruct((rows, width // ny), BF)] * ny,
        cost_estimate=cost(0, 4 * rows * width + 4 * quarter * width),
        compiler_params=pltpu.CompilerParams(vmem_limit_bytes=ROOM),
        name="prepare",
    )(info, far(cot), far(weight), far(weight))


def weight_grad_kernel(count, info, *refs):
    lefts, rights, (give, keep) = refs[:count], refs[count : 2 * count], refs[2 * count :]
    core = info[6]
    tile = 512
    for out, which in ((give, 1 - core), (keep, core)):
        for t in range(0, out.shape[1], tile):
            cols = slice(t, t + tile)
            value = mm(lefts[0][which], rights[0][:, cols])
            for left, right in zip(lefts[1:], rights[1:]):
                value += mm(left[which], right[:, cols])
            out[:, cols] = value.astype(out.dtype)


def weight_grad(info, lefts, rights):
    _, height, tokens = lefts[0].shape
    cols = rights[0].shape[1]
    count = len(lefts)
    return pl.pallas_call(
        functools.partial(weight_grad_kernel, count),
        in_specs=[SM] + [VM] * (2 * count),
        out_specs=[VM, VM],
        out_shape=[
            jax.ShapeDtypeStruct((height, cols), BF),
            jax.ShapeDtypeStruct((height, cols), F32),
        ],
        cost_estimate=cost(
            4 * height * cols * tokens * count, 2 * count * tokens * (2 * height + cols)
        ),
        compiler_params=pltpu.CompilerParams(vmem_limit_bytes=ROOM),
        name="weight_grad",
    )(info, *lefts, *rights)


def join_kernel(info, keep, got, *outs):
    depth = outs[0].shape[0]
    for r, out in enumerate(outs):
        rows = pl.ds(pl.multiple_of((info[2] ^ r) * depth, depth), depth)
        out[...] = (keep[rows] + got[rows].astype(F32)).astype(out.dtype)


def join(info, keep, got, pieces):
    height, cols = keep.shape
    shape = (height // pieces, cols)
    return pl.pallas_call(
        join_kernel,
        in_specs=[SM, VM, VM],
        out_specs=[VM] * pieces,
        out_shape=[jax.ShapeDtypeStruct(shape, F32 if r == 0 else BF) for r in range(pieces)],
        cost_estimate=cost(height * cols, 8 * height * cols),
        compiler_params=pltpu.CompilerParams(vmem_limit_bytes=ROOM),
        name="join",
    )(info, keep, got)


def finish_kernel(counts, backs, heads, spots, factor, info, *refs):
    owns, refs = refs[: len(counts)], refs[len(counts) :]
    returned, refs = refs[: len(backs)], refs[len(backs) :]
    finals, outs, weight_ref = refs[:-3], refs[-3:-1], refs[-1]
    depth, cols = finals[0].shape
    for i, piece in enumerate(finals):
        row = pl.multiple_of(info[spots + 2 * i] * depth, depth)
        col = pl.multiple_of(info[spots + 2 * i + 1] * cols, cols)
        weight_ref[pl.ds(row, depth), pl.ds(col, cols)] = piece[...].astype(F32) * factor
    places = [(b, i) for b, count in enumerate(backs) for i in range(count)]
    u = 0
    for own, count in zip(owns, counts):
        for i in range(count):
            lanes = pl.ds(pl.multiple_of(info[heads + u] * DH, DH), DH)
            b, at = places[u]
            for which, out in enumerate(outs):
                value = own[i, which] + returned[b][at, which].astype(F32)
                out[:, lanes] = value.astype(BF)
            u += 1


def finish(info, heads, spots, factor, owns, returned, finals, shape):
    rows = owns[0].shape[2]
    counts = tuple(own.shape[0] for own in owns)
    backs = tuple(back.shape[0] for back in returned)
    return pl.pallas_call(
        functools.partial(finish_kernel, counts, backs, heads, spots, factor),
        in_specs=[SM] + [VM] * (len(owns) + len(returned) + len(finals)),
        out_specs=[VM, VM, VM],
        out_shape=[jax.ShapeDtypeStruct((rows, sum(counts) * DH), BF)] * 2
        + [jax.ShapeDtypeStruct(shape, F32)],
        cost_estimate=cost(shape[0] * shape[1], 7 * shape[0] * shape[1]),
        compiler_params=pltpu.CompilerParams(vmem_limit_bytes=ROOM),
        name="finish",
    )(info, *owns, *returned, *finals)


def far(value):
    return pltpu.with_memory_space_constraint(value, pltpu.HBM)


def ints(values):
    return jnp.stack([jnp.asarray(v, jnp.int32) for v in values])


def body(queries, key_heads, value_heads, doc_lengths, out_weight, cotangent):
    packs_here, rows, _ = queries.shape
    assert packs_here == 1
    query, keys, values, cot = queries[0], key_heads[0], value_heads[0], cotangent[0]
    n = lax.axis_size("dp")
    m = lax.axis_size("seq")
    ny = m // 4
    split = n // HK
    assert m % 8 == 0 and n == HK * split and split & (split - 1) == 0
    d = lax.axis_index("dp")
    s = lax.axis_index("seq")
    core, x, y = s & 1, (s >> 1) & 1, s >> 2
    top = (s >= m // 2).astype(jnp.int32)

    def along(value, to):
        return lax.ppermute(value, "seq", [(i, to(i)) for i in range(m)])

    def across(value, k):
        return lax.ppermute(value, "dp", [(i, i ^ k) for i in range(n)])

    def swap(value):
        return along(value, lambda i: i ^ 1)

    pair = both(keys, values)
    early = lax.ppermute(pair, "seq", [(i, i + 1) for i in range(m - 1)])

    height, _ = out_weight.shape
    bit = jnp.where(core == 0, top, x)
    other = jnp.where(core == 0, x, top)
    share = lambda i: i ^ (m // 2) if i % 2 == 0 else i ^ 2
    pairs_of = [(k, k + 1) for k in range(1, n - 1, 2)]
    turns = [0, HK - 1, *range(1, HK - 1)] if split == 1 else list(range(HK))
    cuts = CUTS if split == 1 else ()
    calls = list(zip((0,) + cuts, cuts + (HK,)))

    numbers = [s * rows, x, d, y, bit, 2 * core + bit, core]
    heads = len(numbers)
    numbers += [(d // split) ^ u for u in turns]

    def spot(k, parts, part, low):
        turn = sum(jnp.where(k // split == u, i, 0) for i, u in enumerate(turns))
        return ((turn - low) * split + (d ^ k) % split) * parts + part, height // parts

    def call_of(k):
        return max(c for c, (low, _) in enumerate(calls) if low <= turns.index(k // split))

    spots = [[] for _ in calls]
    lows = [low for low, _ in calls]
    spots[0].append(spot(0, 1, 0, 0))
    for k1, k2 in pairs_of:
        c = call_of(k1)
        assert c == call_of(k2)
        mine, theirs = jnp.where(core == 0, k1, k2), jnp.where(core == 0, k2, k1)
        spots[c] += [spot(mine, 2, bit, lows[c]), spot(mine, 2, 1 - bit, lows[c])]
        spots[c] += [spot(theirs, 2, other, lows[c]), spot(theirs, 2, 1 - other, lows[c])]
    c = call_of(n - 1)
    spots[c] += [spot(n - 1, 4, 2 * core + b, lows[c]) for b in (bit, 1 - bit)]
    spots[c] += [spot(n - 1, 4, 2 * (1 - core) + b, lows[c]) for b in (other, 1 - other)]
    spots_at = []
    for row in spots:
        spots_at.append(len(numbers))
        numbers += [v for v, _ in row]
    whole_at = len(numbers)
    for row, low in zip(spots, lows):
        numbers += [v + low * GW // size for v, size in row]
    spread_at = len(numbers)
    for dy in range(ny):
        for dx in range(2):
            spot_y, spot_x = (y + dy) % ny, x ^ dx
            numbers += [2 * spot_x + core, spot_y, 2 * spot_x + 1 - core, spot_y]
    info = ints(numbers)

    half, fourth, *columns = prepare(info, cot, out_weight, ny)

    pieces = [[] for _ in calls]
    pieces[0].append(out_weight)
    for k1, k2 in pairs_of:
        taken = lax.ppermute(
            half, ("seq", "dp"),
            [(a * n + b, a * n + (b ^ (k2 if a % 2 else k1))) for a in range(m) for b in range(n)],
        )
        more = along(taken, share)
        pieces[call_of(k1)] += [taken, more, swap(taken), swap(more)]
    taken = across(fourth, n - 1)
    more = along(taken, share)
    pieces[call_of(n - 1)] += [taken, more, swap(taken), swap(more)]

    rights = {}
    for dy in range(ny):
        here = columns[dy]
        if dy:
            here = along(here, lambda i, dy=dy: (i - 4 * dy) % m)
        rights[dy, 0] = here
        rights[dy, 1] = along(here, lambda i: i ^ 2)

    att, probs, *sets = forward(split, doc_lengths, info, query, early, keys, values)
    lefts = {(0, 0): sets[0], (0, 1): along(sets[1], lambda i: i ^ 2)}
    for dy in range(1, ny):
        for r in range(2):
            lefts[dy, r] = along(lefts[0, r], lambda i, dy=dy: (i - 4 * dy) % m)
    names = sorted(lefts)
    give, keep = weight_grad(
        info, [lefts[name] for name in names], [rights[name] for name in names]
    )
    got = swap(give)
    total, *sums = join(info, keep, got, n)
    for k, part in enumerate(sums, 1):
        total = total + across(part, k).astype(F32)
    final = total.astype(BF)
    finals = []
    for dy in range(ny):
        for dx in range(2):
            to = lambda i, dx=dx, dy=dy: ((i ^ (2 * dx)) - 4 * dy) % m
            here = along(final, to) if dx or dy else final
            finals += [here, swap(here)]
    factor = 1.0 / math.sqrt(n * rows * m)

    owns, returned = [], []
    homeward = [(i, i - 1) for i in range(1, m)]
    links, skip = (), 0
    for c, (low, high) in enumerate(calls):
        last = high == HK
        count = HK - low if last else lows[-1]
        skip = low if last else 0
        grad_query, back, own = units(
            info, heads, spots_at[c], low, high, skip, count, cot, query, early, keys, values,
            probs, pieces[c], links,
        )
        owns.append(own)
        if c >= len(calls) - 2:
            returned.append(lax.ppermute(back, "seq", homeward))
        links = (grad_query,) if c == len(calls) - 2 else (grad_query, back)
    projected = project(info, heads, whole_at, att, [p for part in pieces for p in part])
    grad_keys, grad_values, grad_weight = finish(
        info, heads, spread_at, factor, owns, returned, finals, out_weight.shape
    )
    return tuple(
        a[None] for a in (projected, grad_query, grad_keys, grad_values)
    ) + (grad_weight,)


CUTS = (1, 2)


def solution(mesh):
    token = P("dp", "seq", None)
    return jax.shard_map(
        body,
        mesh=mesh,
        in_specs=(token, token, token, P("dp", None), P("dp", None), token),
        out_specs=(token, token, token, token, P("dp", None)),
        check_vma=False,
    )
```

```python
import functools
import math

import jax
import jax.numpy as jnp
from jax import lax
from jax.experimental import pallas as pl
from jax.experimental.pallas import tpu as pltpu
from jax.sharding import PartitionSpec as P


HQ = 16
HK = 4
DH = 128
GROUP = HQ // HK
GW = GROUP * DH


BF = jnp.bfloat16
ROOM = 24 << 20
F32 = jnp.float32
ANY = pl.BlockSpec(memory_space=pl.ANY)
VM = pl.BlockSpec(memory_space=pltpu.VMEM)
SM = pl.BlockSpec(memory_space=pltpu.SMEM)


def mm(a, b):
    return jnp.dot(a, b, preferred_element_type=F32)


def mm_nt(a, b):
    return lax.dot_general(a, b, (((1,), (1,)), ((), ())), preferred_element_type=F32)


def mm_tn(a, b):
    return lax.dot_general(a, b, (((0,), (0,)), ((), ())), preferred_element_type=F32)


def cost(flops, nbytes, trans=0):
    return pl.CostEstimate(flops=int(flops), bytes_accessed=int(nbytes), transcendentals=int(trans))


def stacked(block, low, size):
    return jnp.concatenate(
        [block[low : low + size, h * DH : (h + 1) * DH] for h in range(GROUP)], axis=0
    )


def forward_kernel(split, lens, place, q_ref, early_ref, k_ref, v_ref, *refs):
    att_ref, p_ref, own, *far_sets, bias, whole = refs
    rows = q_ref.shape[0]
    half = rows // 2
    span = rows + half

    @pl.when(pl.program_id(0) == 0)
    def _():
        for a in range(2):
            base = place[0] + a * half
            q_pos = base + lax.broadcasted_iota(jnp.int32, (span, half), 1)
            k_pos = base - rows + lax.broadcasted_iota(jnp.int32, (span, half), 0)
            begin = jnp.zeros((span, half), jnp.int32)
            opening = jnp.int32(0)
            for i in range(lens.shape[1]):
                begin = jnp.where(opening <= q_pos, opening, begin)
                opening = opening + lens[0, i]
            allowed = (k_pos >= begin) & (k_pos <= q_pos)
            bias[a] = jnp.where(allowed, 0.0, -jnp.inf).astype(F32)

    keys = jnp.concatenate([early_ref[0], k_ref[...]], axis=0)
    values = jnp.concatenate([early_ref[1], v_ref[...]], axis=0)
    block = q_ref[...]
    factor = math.log2(math.e) / math.sqrt(DH)
    for a in range(2):
        part = slice(a * half, a * half + span)
        s = mm_nt(keys[part], stacked(block, a * half, half))
        s = s + jnp.concatenate([bias[a]] * GROUP, axis=1)
        e = jnp.exp2((s - jnp.max(s, axis=0, keepdims=True)) * factor)
        p = (e * (1.0 / jnp.sum(e, axis=0, keepdims=True))).astype(BF)
        p_ref[0, a] = p
        out_t = mm_tn(values[part], p)
        for h in range(GROUP):
            piece = out_t[:, h * half : (h + 1) * half]
            whole[h * DH : (h + 1) * DH, a * half : (a + 1) * half] = piece.astype(BF)
            att_ref[a * half : (a + 1) * half, h * DH : (h + 1) * DH] = piece.T.astype(BF)
    height = GW // split
    quarter = height // 4
    for j in range(2):
        for t in range(split):
            rows_to = slice(t * quarter, (t + 1) * quarter)
            for far_x, out in enumerate((own.at[j], far_sets[j])):
                at = t * height + (2 * (place[1] ^ far_x) + (place[6] ^ j)) * quarter
                out[rows_to] = whole[pl.ds(pl.multiple_of(at, quarter), quarter)]


def forward(split, lens, place, query, early, keys, values):
    rows, width = query.shape
    span = rows + rows // 2
    head = lambda g: (0, g)
    thin = pl.BlockSpec((rows, DH), head)
    return pl.pallas_call(
        functools.partial(forward_kernel, split),
        grid=(HK,),
        in_specs=[
            SM,
            SM,
            pl.BlockSpec((rows, GW), head),
            pl.BlockSpec((2, rows, DH), lambda g: (0, 0, g)),
            thin,
            thin,
        ],
        out_specs=[
            pl.BlockSpec((rows, GW), head),
            pl.BlockSpec((1, 2, span, GW), lambda g: (g, 0, 0, 0)),
        ]
        + [pl.BlockSpec((2, GW // 4, rows), lambda g: (0, g, 0))]
        + [pl.BlockSpec((GW // 4, rows), lambda g: (g, 0))] * 2,
        out_shape=[
            jax.ShapeDtypeStruct(query.shape, BF),
            jax.ShapeDtypeStruct((HK, 2, span, GW), BF),
        ]
        + [jax.ShapeDtypeStruct((2, width // 4, rows), BF)]
        + [jax.ShapeDtypeStruct((width // 4, rows), BF)] * 2,
        scratch_shapes=[pltpu.VMEM((2, span, rows // 2), F32), pltpu.VMEM((GW, rows), BF)],
        cost_estimate=cost(4 * HK * 2 * span * GW * DH, 8 << 20, HK * 2 * span * GW),
        compiler_params=pltpu.CompilerParams(vmem_limit_bytes=ROOM),
        name="attend_forward",
    )(lens, place, far(query), early, far(keys), far(values))


def units_kernel(sizes, spots, info, cot_ref, q_ref, early_ref, k_ref, v_ref, p_ref, *refs):
    pieces = refs[: len(sizes)]
    dq_ref, back_ref, own_ref, weights, sems = refs[-5:]
    step = pl.program_id(0)

    @pl.when(step == 0)
    def _():
        copies = []
        for i, size in enumerate(sizes):
            spot = pl.multiple_of(info[spots + i] * size, size)
            copies.append(
                pltpu.make_async_copy(pieces[i], weights.at[pl.ds(spot, size)], sems.at[i])
            )
        for copy in copies:
            copy.start()
        for copy in copies:
            copy.wait()

    weight = weights.at[pl.ds(pl.multiple_of(step * GW, GW), GW)]
    rows = q_ref.shape[0]
    half = rows // 2
    span = rows + half
    scale = 1.0 / math.sqrt(DH)
    grads = mm_nt(cot_ref[...], weight[...]).astype(BF)
    keys = jnp.concatenate([early_ref[0], k_ref[...]], axis=0)
    values = jnp.concatenate([early_ref[1], v_ref[...]], axis=0)
    block = q_ref[...]
    key_parts, value_parts = [], []
    for a in range(2):
        part = slice(a * half, a * half + span)
        qs, gs = stacked(block, a * half, half), stacked(grads, a * half, half)
        low = p_ref[0, a]
        p = low.astype(F32)
        dp = mm_nt(values[part], gs)
        delta = jnp.sum(p * dp, axis=0, keepdims=True)
        ds = (p * (dp - delta)).astype(BF)
        key_parts.append(mm(ds, qs) * scale)
        value_parts.append(mm(low, gs))
        out_t = mm_tn(keys[part], ds) * scale
        for h in range(GROUP):
            piece = out_t[:, h * half : (h + 1) * half]
            dq_ref[a * half : (a + 1) * half, h * DH : (h + 1) * DH] = piece.T.astype(BF)
    for which, (early, late) in enumerate((key_parts, value_parts)):
        back_ref[0, which, :half] = early[:half].astype(BF)
        back_ref[0, which, half:] = (early[half:rows] + late[:half]).astype(BF)
        own_ref[0, which, :half] = early[rows:] + late[half:rows]
        own_ref[0, which, half:] = late[rows:]


def units(
    info, heads, spots, low, high, skip, count, cot, query, early, keys, values, probs, pieces,
    links
):
    rows, width = cot.shape
    span = rows + rows // 2
    steps = high - low
    head = lambda i, w: w[heads + low + i]
    full = pl.BlockSpec((rows, width), lambda i, w: (0, 0))
    wide = pl.BlockSpec((rows, GW), lambda i, w: (0, head(i, w)))
    thin = pl.BlockSpec((rows, DH), lambda i, w: (0, head(i, w)))
    pair = pl.BlockSpec((1, 2, rows, DH), lambda i, w: (i, 0, 0, 0))
    later = pl.BlockSpec((1, 2, rows, DH), lambda i, w: (i + low - skip, 0, 0, 0))
    both = pl.BlockSpec((2, rows, DH), lambda i, w: (0, 0, head(i, w)))
    sizes = tuple(piece.shape[0] for piece in pieces)
    return pl.pallas_call(
        functools.partial(units_kernel, sizes, spots),
        grid_spec=pltpu.PrefetchScalarGridSpec(
            num_scalar_prefetch=1,
            grid=(steps,),
            in_specs=[full, wide, both, thin, thin]
            + [pl.BlockSpec((1, 2, span, GW), lambda i, w: (head(i, w), 0, 0, 0))]
            + [ANY] * (len(pieces) + len(links)),
            out_specs=[wide, later, pair],
            scratch_shapes=[
                pltpu.VMEM((steps * GW, width), BF),
                pltpu.SemaphoreType.DMA((len(pieces),)),
            ],
        ),
        out_shape=[
            jax.ShapeDtypeStruct(query.shape, BF),
            jax.ShapeDtypeStruct((count, 2, rows, DH), BF),
            jax.ShapeDtypeStruct((steps, 2, rows, DH), F32),
        ],
        input_output_aliases={7 + len(pieces) + i: i for i in range(len(links))},
        cost_estimate=cost(
            steps * (2 * rows * GW * width + 8 * 2 * span * GW * DH), steps * (5 << 20)
        ),
        compiler_params=pltpu.CompilerParams(vmem_limit_bytes=ROOM),
        name="units",
    )(info, far(cot), far(query), early, far(keys), far(values), probs, *pieces, *links)


def project_kernel(sizes, heads, spots, info, att_ref, *refs):
    pieces, (out_ref, weights, sems) = refs[: len(sizes)], refs[len(sizes) :]
    copies = []
    for i, size in enumerate(sizes):
        spot = pl.multiple_of(info[spots + i] * size, size)
        copies.append(
            pltpu.make_async_copy(pieces[i], weights.at[pl.ds(spot, size)], sems.at[i])
        )
    for copy in copies:
        copy.start()
    for copy in copies:
        copy.wait()
    lefts = [
        att_ref[:, pl.ds(pl.multiple_of(info[heads + u] * GW, GW), GW)] for u in range(HK)
    ]
    tile = 512
    for t in range(0, out_ref.shape[1], tile):
        value = mm(lefts[0], weights[:GW, t : t + tile])
        for u in range(1, HK):
            value += mm(lefts[u], weights[u * GW : (u + 1) * GW, t : t + tile])
        out_ref[:, t : t + tile] = value.astype(BF)


def project(info, heads, spots, att, pieces):
    rows, depth = att.shape
    width = pieces[0].shape[1]
    sizes = tuple(piece.shape[0] for piece in pieces)
    return pl.pallas_call(
        functools.partial(project_kernel, sizes, heads, spots),
        in_specs=[SM, VM] + [ANY] * len(pieces),
        out_specs=VM,
        out_shape=jax.ShapeDtypeStruct((rows, width), BF),
        scratch_shapes=[
            pltpu.VMEM((depth, width), BF),
            pltpu.SemaphoreType.DMA((len(pieces),)),
        ],
        cost_estimate=cost(2 * rows * depth * width, 2 * width * (depth + rows)),
        compiler_params=pltpu.CompilerParams(vmem_limit_bytes=ROOM),
        name="project",
    )(info, att, *pieces)


def both_kernel(k_ref, v_ref, out_ref):
    out_ref[0] = k_ref[...]
    out_ref[1] = v_ref[...]


def both(keys, values):
    return pl.pallas_call(
        both_kernel,
        in_specs=[VM, VM],
        out_specs=VM,
        out_shape=jax.ShapeDtypeStruct((2,) + keys.shape, BF),
        cost_estimate=cost(0, 8 * keys.size),
        compiler_params=pltpu.CompilerParams(vmem_limit_bytes=ROOM),
        name="both",
    )(far(keys), far(values))


def prepare_kernel(info, cot_ref, half_ref, quarter_ref, *outs):
    outs[0][...] = half_ref[...]
    outs[1][...] = quarter_ref[...]
    cols = outs[2].shape[1]
    count = len(outs) - 2
    for dy, out in enumerate(outs[2:]):
        which = lax.rem(info[3] + count - dy, count)
        out[...] = cot_ref[:, pl.ds(pl.multiple_of(which * cols, cols), cols)]


def prepare(info, cot, weight, ny):
    rows, width = cot.shape
    half, quarter = weight.shape[0] // 2, weight.shape[0] // 4
    still = lambda i, w: (0, 0)
    return pl.pallas_call(
        prepare_kernel,
        grid_spec=pltpu.PrefetchScalarGridSpec(
            num_scalar_prefetch=1,
            grid=(1,),
            in_specs=[
                pl.BlockSpec((rows, width), still),
                pl.BlockSpec((half, width), lambda i, w: (w[4], 0)),
                pl.BlockSpec((quarter, width), lambda i, w: (w[5], 0)),
            ],
            out_specs=[
                pl.BlockSpec((half, width), still),
                pl.BlockSpec((quarter, width), still),
            ]
            + [pl.BlockSpec((rows, width // ny), still)] * ny,
        ),
        out_shape=[
            jax.ShapeDtypeStruct((half, width), BF),
            jax.ShapeDtypeStruct((quarter, width), BF),
        ]
        + [jax.ShapeDtypeStruct((rows, width // ny), BF)] * ny,
        cost_estimate=cost(0, 4 * rows * width + 4 * quarter * width),
        compiler_params=pltpu.CompilerParams(vmem_limit_bytes=ROOM),
        name="prepare",
    )(info, far(cot), far(weight), far(weight))


def weight_grad_kernel(count, info, *refs):
    near, far_keep, far_give, rights = [refs[i * count : (i + 1) * count] for i in range(3)] + [
        refs[3 * count : 5 * count]
    ]
    give, keep = refs[5 * count :]
    tile = 512
    for out, j, beyond in ((give, 1, far_give), (keep, 0, far_keep)):
        lefts = [left[j] for left in near] + [left[...] for left in beyond]
        for t in range(0, out.shape[1], tile):
            cols = slice(t, t + tile)
            value = mm(lefts[0], rights[0][:, cols])
            for left, right in zip(lefts[1:], rights[1:]):
                value += mm(left, right[:, cols])
            out[:, cols] = value.astype(out.dtype)


def weight_grad(info, near, far_keep, far_give, rights):
    _, height, tokens = near[0].shape
    cols = rights[0].shape[1]
    count = len(near)
    return pl.pallas_call(
        functools.partial(weight_grad_kernel, count),
        in_specs=[SM] + [VM] * (5 * count),
        out_specs=[VM, VM],
        out_shape=[
            jax.ShapeDtypeStruct((height, cols), BF),
            jax.ShapeDtypeStruct((height, cols), F32),
        ],
        cost_estimate=cost(
            8 * height * cols * tokens * count, 4 * count * tokens * (2 * height + cols)
        ),
        compiler_params=pltpu.CompilerParams(vmem_limit_bytes=ROOM),
        name="weight_grad",
    )(info, *near, *far_keep, *far_give, *rights)


def join_kernel(info, keep, got, *outs):
    depth = outs[0].shape[0]
    for r, out in enumerate(outs):
        rows = pl.ds(pl.multiple_of((info[2] ^ r) * depth, depth), depth)
        out[...] = (keep[rows] + got[rows].astype(F32)).astype(out.dtype)


def join(info, keep, got, pieces):
    height, cols = keep.shape
    shape = (height // pieces, cols)
    return pl.pallas_call(
        join_kernel,
        in_specs=[SM, VM, VM],
        out_specs=[VM] * pieces,
        out_shape=[jax.ShapeDtypeStruct(shape, F32 if r == 0 else BF) for r in range(pieces)],
        cost_estimate=cost(height * cols, 8 * height * cols),
        compiler_params=pltpu.CompilerParams(vmem_limit_bytes=ROOM),
        name="join",
    )(info, keep, got)


def finish_kernel(counts, backs, heads, spots, factor, info, *refs):
    owns, refs = refs[: len(counts)], refs[len(counts) :]
    returned, refs = refs[: len(backs)], refs[len(backs) :]
    finals, outs, weight_ref = refs[:-3], refs[-3:-1], refs[-1]
    depth, cols = finals[0].shape
    for i, piece in enumerate(finals):
        row = pl.multiple_of(info[spots + 2 * i] * depth, depth)
        col = pl.multiple_of(info[spots + 2 * i + 1] * cols, cols)
        weight_ref[pl.ds(row, depth), pl.ds(col, cols)] = piece[...].astype(F32) * factor
    places = [(b, i) for b, count in enumerate(backs) for i in range(count)]
    u = 0
    for own, count in zip(owns, counts):
        for i in range(count):
            lanes = pl.ds(pl.multiple_of(info[heads + u] * DH, DH), DH)
            b, at = places[u]
            for which, out in enumerate(outs):
                value = own[i, which] + returned[b][at, which].astype(F32)
                out[:, lanes] = value.astype(BF)
            u += 1


def finish(info, heads, spots, factor, owns, returned, finals, shape):
    rows = owns[0].shape[2]
    counts = tuple(own.shape[0] for own in owns)
    backs = tuple(back.shape[0] for back in returned)
    return pl.pallas_call(
        functools.partial(finish_kernel, counts, backs, heads, spots, factor),
        in_specs=[SM] + [VM] * (len(owns) + len(returned) + len(finals)),
        out_specs=[VM, VM, VM],
        out_shape=[jax.ShapeDtypeStruct((rows, sum(counts) * DH), BF)] * 2
        + [jax.ShapeDtypeStruct(shape, F32)],
        cost_estimate=cost(shape[0] * shape[1], 7 * shape[0] * shape[1]),
        compiler_params=pltpu.CompilerParams(vmem_limit_bytes=ROOM),
        name="finish",
    )(info, *owns, *returned, *finals)


def far(value):
    return pltpu.with_memory_space_constraint(value, pltpu.HBM)


def ints(values):
    return jnp.stack([jnp.asarray(v, jnp.int32) for v in values])


def body(queries, key_heads, value_heads, doc_lengths, out_weight, cotangent):
    packs_here, rows, _ = queries.shape
    assert packs_here == 1
    query, keys, values, cot = queries[0], key_heads[0], value_heads[0], cotangent[0]
    n = lax.axis_size("dp")
    m = lax.axis_size("seq")
    ny = m // 4
    split = n // HK
    assert m % 8 == 0 and n == HK * split and split & (split - 1) == 0
    d = lax.axis_index("dp")
    s = lax.axis_index("seq")
    core, x, y = s & 1, (s >> 1) & 1, s >> 2
    top = (s >= m // 2).astype(jnp.int32)

    def along(value, to):
        return lax.ppermute(value, "seq", [(i, to(i)) for i in range(m)])

    def across(value, k):
        return lax.ppermute(value, "dp", [(i, i ^ k) for i in range(n)])

    def swap(value):
        return along(value, lambda i: i ^ 1)

    pair = both(keys, values)
    early = lax.ppermute(pair, "seq", [(i, i + 1) for i in range(m - 1)])

    height, _ = out_weight.shape
    bit = jnp.where(core == 0, top, x)
    other = jnp.where(core == 0, x, top)
    share = lambda i: i ^ (m // 2) if i % 2 == 0 else i ^ 2
    pairs_of = [(k, k + 1) for k in range(1, n - 1, 2)]
    turns = [0, HK - 1, *range(1, HK - 1)] if split == 1 else list(range(HK))
    cuts = CUTS if split == 1 else ()
    calls = list(zip((0,) + cuts, cuts + (HK,)))

    numbers = [s * rows, x, d, y, bit, 2 * core + bit, core]
    heads = len(numbers)
    numbers += [(d // split) ^ u for u in turns]

    def spot(k, parts, part, low):
        turn = sum(jnp.where(k // split == u, i, 0) for i, u in enumerate(turns))
        return ((turn - low) * split + (d ^ k) % split) * parts + part, height // parts

    def call_of(k):
        return max(c for c, (low, _) in enumerate(calls) if low <= turns.index(k // split))

    spots = [[] for _ in calls]
    lows = [low for low, _ in calls]
    spots[0].append(spot(0, 1, 0, 0))
    for k1, k2 in pairs_of:
        c = call_of(k1)
        assert c == call_of(k2)
        mine, theirs = jnp.where(core == 0, k1, k2), jnp.where(core == 0, k2, k1)
        spots[c] += [spot(mine, 2, bit, lows[c]), spot(mine, 2, 1 - bit, lows[c])]
        spots[c] += [spot(theirs, 2, other, lows[c]), spot(theirs, 2, 1 - other, lows[c])]
    c = call_of(n - 1)
    spots[c] += [spot(n - 1, 4, 2 * core + b, lows[c]) for b in (bit, 1 - bit)]
    spots[c] += [spot(n - 1, 4, 2 * (1 - core) + b, lows[c]) for b in (other, 1 - other)]
    spots_at = []
    for row in spots:
        spots_at.append(len(numbers))
        numbers += [v for v, _ in row]
    whole_at = len(numbers)
    for row, low in zip(spots, lows):
        numbers += [v + low * GW // size for v, size in row]
    spread_at = len(numbers)
    for dy in range(ny):
        for dx in range(2):
            spot_y, spot_x = (y + dy) % ny, x ^ dx
            numbers += [2 * spot_x + core, spot_y, 2 * spot_x + 1 - core, spot_y]
    info = ints(numbers)

    half, fourth, *columns = prepare(info, cot, out_weight, ny)

    pieces = [[] for _ in calls]
    pieces[0].append(out_weight)
    for k1, k2 in pairs_of:
        taken = lax.ppermute(
            half, ("seq", "dp"),
            [(a * n + b, a * n + (b ^ (k2 if a % 2 else k1))) for a in range(m) for b in range(n)],
        )
        more = along(taken, share)
        pieces[call_of(k1)] += [taken, more, swap(taken), swap(more)]
    taken = across(fourth, n - 1)
    more = along(taken, share)
    pieces[call_of(n - 1)] += [taken, more, swap(taken), swap(more)]

    rights = {}
    for dy in range(ny):
        here = columns[dy]
        if dy:
            here = along(here, lambda i, dy=dy: (i - 4 * dy) % m)
        rights[dy, 0] = here
        rights[dy, 1] = along(here, lambda i: i ^ 2)

    att, probs, own, *others = forward(split, doc_lengths, info, query, early, keys, values)
    near, fars = [own], [[along(others[j], lambda i: i ^ 2)] for j in range(2)]
    for dy in range(1, ny):
        shift = lambda i, dy=dy: (i - 4 * dy) % m
        near.append(along(own, shift))
        for j in range(2):
            fars[j].append(along(fars[j][0], shift))
    give, keep = weight_grad(
        info, near, *fars, [rights[dy, r] for r in range(2) for dy in range(ny)]
    )
    got = swap(give)
    total, *sums = join(info, keep, got, n)
    for k, part in enumerate(sums, 1):
        total = total + across(part, k).astype(F32)
    final = total.astype(BF)
    finals = []
    for dy in range(ny):
        for dx in range(2):
            to = lambda i, dx=dx, dy=dy: ((i ^ (2 * dx)) - 4 * dy) % m
            here = along(final, to) if dx or dy else final
            finals += [here, swap(here)]
    factor = 1.0 / math.sqrt(n * rows * m)

    owns, returned = [], []
    homeward = [(i, i - 1) for i in range(1, m)]
    links, skip = (), 0
    for c, (low, high) in enumerate(calls):
        last = high == HK
        count = HK - low if last else lows[-1]
        skip = low if last else 0
        grad_query, back, own = units(
            info, heads, spots_at[c], low, high, skip, count, cot, query, early, keys, values,
            probs, pieces[c], links,
        )
        owns.append(own)
        if c >= len(calls) - 2:
            returned.append(lax.ppermute(back, "seq", homeward))
        links = (grad_query,) if c == len(calls) - 2 else (grad_query, back)
    projected = project(info, heads, whole_at, att, [p for part in pieces for p in part])
    grad_keys, grad_values, grad_weight = finish(
        info, heads, spread_at, factor, owns, returned, finals, out_weight.shape
    )
    return tuple(
        a[None] for a in (projected, grad_query, grad_keys, grad_values)
    ) + (grad_weight,)


CUTS = (1, 2)


def solution(mesh):
    token = P("dp", "seq", None)
    return jax.shard_map(
        body,
        mesh=mesh,
        in_specs=(token, token, token, P("dp", None), P("dp", None), token),
        out_specs=(token, token, token, token, P("dp", None)),
        check_vma=False,
    )
```
